32 devices in a mesh: phase: 4 (over y, core), row: 8 (over z, x).
Axes of the slice: x: 2, y: 2, z: 4, core: 2. Of those that a mesh axis runs over, the one named last changes fastest.
Arguments:
- linkage: float32 [2, 4, 1024, 1024], P(None, 'phase', 'row'), as said below
- pulse: float32 [32, 5, 3], replicated, may hold values from -1.2 to 1.2
- segments: int32 [4, 2], P('phase'), may hold values from 0 to 31
- ticks: int32 [4, 2], P('phase'), may hold values from 1 to 4
- detuning: float32 [5], replicated, may hold values from -0.4 to 0.4
- level_shift: float32 [5], replicated, may hold values from -1 to 1
- coupling: float32 [4], replicated, may hold values from -0.5 to 0.5
- dephase: float32 [5], replicated, may hold values from 0.01 to 0.1
Outputs:
- link_gradient: float32 [2, 4, 1024, 1024], P(None, 'phase', 'row')
The draws below stay inside these ranges and needn't reach their ends.
Inputs may be any that keep to these rules, and one draw needn't show every extreme that they name: Every linkage state is Hermitian: for each phase, the real part is a symmetric matrix and the imaginary part an antisymmetric one.
All inputs are finite; a program needn't handle non-finite values.
Results may differ from the reference program's by a relative error of at most 0.0003.
Values sent between devices are 32-bit elements; how exact they have to be, the bound alone decides.
A program may use at most 64 MiB of HBM per device.

```python
import math
import jax
import jax.numpy as jnp
from jax import lax

TRANSMONS = 5
LEVELS = 4
STEPS = 2
SEGMENTS = 32
ORDER = 1024
HALF = 2
PHASES = 4


def draw_linkage(key, part):
    first_key = jax.random.fold_in(key, 11)
    second_key = jax.random.fold_in(key, 23)
    real_draw = jax.random.normal(first_key, (PHASES, ORDER, ORDER), jnp.float32)
    imag_draw = jax.random.normal(second_key, (PHASES, ORDER, ORDER), jnp.float32)
    real_component = (real_draw + jnp.swapaxes(real_draw, 1, 2)) * 0.7071067811865476
    imaginary_component = (imag_draw - jnp.swapaxes(imag_draw, 1, 2)) * 0.7071067811865476
    return jnp.stack([real_component, imaginary_component]).astype(jnp.float32)


def plant(array, rng, least, largest):
    spot = [jax.random.randint(jax.random.fold_in(rng, axis), (), 0, length) for axis, length in enumerate(array.shape)]
    main_axis = array.shape.index(max(array.shape))
    beside = spot[:main_axis] + [(spot[main_axis] + 1) % array.shape[main_axis]] + spot[main_axis + 1:]
    return array.at[tuple(spot)].set(least).at[tuple(beside)].set(largest)


def setup_inputs(seed: int = 0) -> dict:
    splits = jax.random.split(jax.random.key(seed), 9)
    linkage = draw_linkage(jax.random.fold_in(splits[8], 71), 0)
    pulse = jnp.clip(jax.random.uniform(splits[1], (SEGMENTS, TRANSMONS, LEVELS - 1), jnp.float32, -1.2, 1.2), -1.2, 1.2)
    segments = plant(jax.random.randint(splits[2], (PHASES, STEPS), 0, SEGMENTS), jax.random.fold_in(splits[2], 1), 0, SEGMENTS - 1).astype(jnp.int32)
    ticks = plant(jax.random.randint(splits[3], (PHASES, STEPS), 1, 5), jax.random.fold_in(splits[3], 1), 1, 4).astype(jnp.int32)
    detuning = jnp.clip(jax.random.uniform(splits[4], (TRANSMONS,), jnp.float32, -0.4, 0.4), -0.4, 0.4)
    level_shift = jnp.clip(jax.random.uniform(splits[5], (TRANSMONS,), jnp.float32, -1.0, 1.0), -1.0, 1.0)
    coupling = jnp.clip(jax.random.uniform(splits[6], (TRANSMONS - 1,), jnp.float32, -0.5, 0.5), -0.5, 0.5)
    dephase = jnp.clip(jnp.exp(jax.random.uniform(splits[7], (TRANSMONS,), jnp.float32, math.log(0.01), math.log(0.1))), 0.01, 0.1)
    return {"linkage": linkage, "pulse": pulse, "segments": segments, "ticks": ticks, "detuning": detuning, "level_shift": level_shift, "coupling": coupling, "dephase": dephase}


TOP_ACCURACY = lax.Precision.HIGHEST


def digits(indices):
    powers = LEVELS ** (TRANSMONS - 1 - jnp.arange(TRANSMONS, dtype=jnp.int32))
    return ((indices[None, :] // powers[:, None]) % LEVELS).astype(jnp.float32)


def energies(levels, level_shift, coupling):
    own_part = jnp.sum(level_shift[:, None] * levels * (levels - 1.0) * 0.5, axis=0)
    return own_part + jnp.sum(coupling[:, None] * levels[:-1] * levels[1:], axis=0)


def drift_tables(row_levels, col_levels, level_shift, coupling, dephase):
    detune_grid = energies(row_levels, level_shift, coupling)[:, None] - energies(col_levels, level_shift, coupling)[None, :]
    weighted = dephase[:, None] * row_levels
    cross = jnp.dot(weighted.T, col_levels, preferred_element_type=jnp.float32, precision=TOP_ACCURACY)
    row_part = jnp.sum(weighted * row_levels, axis=0)
    col_part = jnp.sum(dephase[:, None] * col_levels * col_levels, axis=0)
    decay = row_part[:, None] + col_part[None, :] - 2.0 * cross
    return decay, detune_grid


def half_factor(decay, detune_grid, span):
    magnitude = jnp.exp(-0.5 * span * decay)
    return magnitude * jnp.cos(0.5 * span * detune_grid), -magnitude * jnp.sin(0.5 * span * detune_grid)


def weigh(field, factor_real, factor_imag):
    return jnp.stack([field[0] * factor_real - field[1] * factor_imag, field[0] * factor_imag + field[1] * factor_real])


def complex_product(left_real_component, left_imaginary, right_real_component, right_imaginary):
    real_component = jnp.einsum('nmx,nxw->nmw', left_real_component, right_real_component, precision=TOP_ACCURACY) - jnp.einsum('nmx,nxw->nmw', left_imaginary, right_imaginary, precision=TOP_ACCURACY)
    imaginary_component = jnp.einsum('nmx,nxw->nmw', left_real_component, right_imaginary, precision=TOP_ACCURACY) + jnp.einsum('nmx,nxw->nmw', left_imaginary, right_real_component, precision=TOP_ACCURACY)
    return real_component, imaginary_component


def rotations(theta, phi):
    identity = jnp.eye(LEVELS, dtype=jnp.float32)
    total_real = jnp.broadcast_to(identity, (theta.shape[0], LEVELS, LEVELS))
    total_imag = jnp.zeros((theta.shape[0], LEVELS, LEVELS), jnp.float32)
    for level in range(LEVELS - 1):
        upper = jnp.outer(identity[level], identity[level + 1])
        lower = upper.T
        block = jnp.outer(identity[level], identity[level]) + jnp.outer(identity[level + 1], identity[level + 1])
        cosine = jnp.cos(theta[:, level])[:, None, None]
        sine = jnp.sin(theta[:, level])[:, None, None]
        phase_cos = jnp.cos(phi[:, level])[:, None, None]
        phase_sin = jnp.sin(phi[:, level])[:, None, None]
        rot_real = identity + (cosine - 1.0) * block + sine * phase_cos * (lower - upper)
        rot_imag = sine * phase_sin * (upper + lower)
        total_real, total_imag = complex_product(total_real, total_imag, rot_real, rot_imag)
    return total_real, total_imag


def kron_range(unit_real, unit_imag, first, last):
    acc_real, acc_imag = unit_real[first], unit_imag[first]
    for transmon in range(first + 1, last):
        next_real, next_imag = unit_real[transmon], unit_imag[transmon]
        acc_real, acc_imag = (jnp.kron(acc_real, next_real) - jnp.kron(acc_imag, next_imag),
                              jnp.kron(acc_real, next_imag) + jnp.kron(acc_imag, next_real))
    return acc_real, acc_imag


def real_form(matrix_real, matrix_imag):
    return jnp.stack([jnp.stack([matrix_real, -matrix_imag], axis=1), jnp.stack([matrix_imag, matrix_real], axis=1)], axis=0)


def factor_forms(unit_real, unit_imag, grouped):
    if grouped:
        pairs = [kron_range(unit_real, unit_imag, 0, HALF), kron_range(unit_real, unit_imag, HALF, TRANSMONS)]
    else:
        pairs = [(unit_real[transmon], unit_imag[transmon]) for transmon in range(TRANSMONS)]
    forward_left = [real_form(matrix_real, matrix_imag) for matrix_real, matrix_imag in pairs]
    forward_right = [real_form(matrix_real, -matrix_imag) for matrix_real, matrix_imag in pairs]
    adjoint_left = [real_form(matrix_real.T, -matrix_imag.T) for matrix_real, matrix_imag in pairs]
    adjoint_right = [real_form(matrix_real.T, matrix_imag.T) for matrix_real, matrix_imag in pairs]
    return forward_left, forward_right, adjoint_left, adjoint_right


def apply_factor(field, form, leading, trailing):
    width = form.shape[3]
    shaped = field.reshape(2, leading, width, trailing)
    result = jnp.einsum('cgdf,dpfq->cpgq', form, shaped, precision=TOP_ACCURACY)
    return result.reshape(field.shape)


def apply_factors(field, forms, leading, trailing):
    widths = [form.shape[3] for form in forms]
    for position, form in enumerate(forms):
        before = math.prod(widths[:position])
        after = math.prod(widths[position + 1:])
        field = apply_factor(field, form, leading * before, after * trailing)
    return field


def step_unitaries(pulse, segment, clock, span, detuning):
    onehot = (jnp.arange(SEGMENTS, dtype=jnp.int32) == segment).astype(jnp.float32)
    theta = jnp.einsum('s,skm->km', onehot, pulse, precision=TOP_ACCURACY)
    multiple = jnp.arange(1, LEVELS, dtype=jnp.int32).astype(jnp.float32)
    phi = detuning[:, None] * (clock + 0.5 * span) * multiple[None, :]
    return rotations(theta, phi)


def full_sandwich(field, left_forms, right_forms):
    field = apply_factors(field, left_forms, 1, ORDER)
    return apply_factors(field, right_forms, ORDER, 1)


def reference(linkage, pulse, segments, ticks, detuning, level_shift, coupling, dephase):
    levels = digits(jnp.arange(ORDER, dtype=jnp.int32))
    decay, detune_grid = drift_tables(levels, levels, level_shift, coupling, dephase)
    totals = jnp.sum(ticks, axis=1, dtype=jnp.int32)
    starts = (jnp.cumsum(totals, dtype=jnp.int32) - totals).astype(jnp.int32)

    def prepared(phase_index, step_index):
        span = ticks[phase_index, step_index].astype(jnp.float32)
        earlier = jnp.sum(ticks[phase_index, :step_index], dtype=jnp.int32)
        clock = (starts[phase_index] + earlier).astype(jnp.float32)
        unit_real, unit_imag = step_unitaries(pulse, segments[phase_index, step_index], clock, span, detuning)
        return span, factor_forms(unit_real, unit_imag, True)

    def forward(phase_index):
        field = linkage[:, phase_index]
        for step_index in range(STEPS):
            span, forms = prepared(phase_index, step_index)
            factor_real, factor_imag = half_factor(decay, detune_grid, span)
            field = weigh(field, factor_real, factor_imag)
            field = full_sandwich(field, forms[0], forms[1])
            field = weigh(field, factor_real, factor_imag)
        return field

    phase_ids = jnp.arange(PHASES, dtype=jnp.int32)
    ends = jnp.moveaxis(lax.map(forward, phase_ids), 0, 1)
    mismatch = ends - jnp.roll(linkage, -1, axis=1)

    def backward(phase_index):
        field = mismatch[:, phase_index]
        for step_index in reversed(range(STEPS)):
            span, forms = prepared(phase_index, step_index)
            factor_real, factor_imag = half_factor(decay, detune_grid, span)
            field = weigh(field, factor_real, -factor_imag)
            field = full_sandwich(field, forms[2], forms[3])
            field = weigh(field, factor_real, -factor_imag)
        return field

    adjoints = jnp.moveaxis(lax.map(backward, phase_ids), 0, 1)
    return adjoints - jnp.roll(mismatch, 1, axis=1)
```

```python
import functools
import math

import jax
import jax.numpy as jnp
from jax import lax
from jax.experimental import pallas as pl
from jax.experimental.pallas import tpu as pltpu
from jax.sharding import PartitionSpec as P

TRANSMONS = 5
LEVELS = 4
STEPS = 2
SEGMENTS = 32
HALF = 2
MESH = pl.DeviceIdType.MESH


TOP_ACCURACY = lax.Precision.HIGHEST


def prefix(value, axis, join, neutral):
    count, mine = (lax.axis_size(axis), lax.axis_index(axis))
    pieces = lax.all_gather(value, axis)
    subtotal = jnp.full_like(value, 0) + jnp.asarray(neutral, value.dtype)

    def lap(position, subtotal):
        longer = join(subtotal, pieces[position])
        return jnp.where(position < mine, longer, subtotal)

    return lax.fori_loop(0, count - 1, lap, subtotal)


def shifted(block, axis, distance):
    devices = range(lax.axis_size(axis))
    route = [((i - distance) % len(devices), i) for i in devices]
    return lax.ppermute(block, axis, route)


def digits(indices):
    powers = LEVELS ** (TRANSMONS - 1 - jnp.arange(TRANSMONS, dtype=jnp.int32))
    return (indices[None, :] // powers[:, None] % LEVELS).astype(jnp.float32)


def energies(levels, level_shift, coupling):
    own_part = jnp.sum(level_shift[:, None] * levels * (levels - 1.0) * 0.5, axis=0)
    return own_part + jnp.sum(coupling[:, None] * levels[:-1] * levels[1:], axis=0)


def drift_tables(row_levels, col_levels, level_shift, coupling, dephase):
    detune_grid = (
        energies(row_levels, level_shift, coupling)[:, None]
        - energies(col_levels, level_shift, coupling)[None, :]
    )
    weighted = dephase[:, None] * row_levels
    cross = jnp.dot(
        weighted.T, col_levels, preferred_element_type=jnp.float32, precision=TOP_ACCURACY
    )
    row_part = jnp.sum(weighted * row_levels, axis=0)
    col_part = jnp.sum(dephase[:, None] * col_levels * col_levels, axis=0)
    decay = row_part[:, None] + col_part[None, :] - 2.0 * cross
    return (decay, detune_grid)


def half_factor(decay, detune_grid, span):
    magnitude = jnp.exp(-0.5 * span * decay)
    return (
        magnitude * jnp.cos(0.5 * span * detune_grid),
        -magnitude * jnp.sin(0.5 * span * detune_grid),
    )


def weigh(field, factor_real, factor_imag):
    return jnp.stack(
        [
            field[0] * factor_real - field[1] * factor_imag,
            field[0] * factor_imag + field[1] * factor_real,
        ]
    )


def complex_product(left_real_component, left_imaginary, right_real_component, right_imaginary):
    real_component = jnp.einsum(
        "nmx,nxw->nmw", left_real_component, right_real_component, precision=TOP_ACCURACY
    ) - jnp.einsum("nmx,nxw->nmw", left_imaginary, right_imaginary, precision=TOP_ACCURACY)
    imaginary_component = jnp.einsum(
        "nmx,nxw->nmw", left_real_component, right_imaginary, precision=TOP_ACCURACY
    ) + jnp.einsum("nmx,nxw->nmw", left_imaginary, right_real_component, precision=TOP_ACCURACY)
    return (real_component, imaginary_component)


def rotations(theta, phi):
    identity = jnp.eye(LEVELS, dtype=jnp.float32)
    total_real = jnp.broadcast_to(identity, (theta.shape[0], LEVELS, LEVELS))
    total_imag = jnp.zeros((theta.shape[0], LEVELS, LEVELS), jnp.float32)
    for level in range(LEVELS - 1):
        upper = jnp.outer(identity[level], identity[level + 1])
        lower = upper.T
        block = jnp.outer(identity[level], identity[level]) + jnp.outer(
            identity[level + 1], identity[level + 1]
        )
        cosine = jnp.cos(theta[:, level])[:, None, None]
        sine = jnp.sin(theta[:, level])[:, None, None]
        phase_cos = jnp.cos(phi[:, level])[:, None, None]
        phase_sin = jnp.sin(phi[:, level])[:, None, None]
        rot_real = identity + (cosine - 1.0) * block + sine * phase_cos * (lower - upper)
        rot_imag = sine * phase_sin * (upper + lower)
        total_real, total_imag = complex_product(total_real, total_imag, rot_real, rot_imag)
    return (total_real, total_imag)


def kron_range(unit_real, unit_imag, first, last):
    acc_real, acc_imag = (unit_real[first], unit_imag[first])
    for transmon in range(first + 1, last):
        next_real, next_imag = (unit_real[transmon], unit_imag[transmon])
        acc_real, acc_imag = (
            jnp.kron(acc_real, next_real) - jnp.kron(acc_imag, next_imag),
            jnp.kron(acc_real, next_imag) + jnp.kron(acc_imag, next_real),
        )
    return (acc_real, acc_imag)


def real_form(matrix_real, matrix_imag):
    return jnp.stack(
        [
            jnp.stack([matrix_real, -matrix_imag], axis=1),
            jnp.stack([matrix_imag, matrix_real], axis=1),
        ],
        axis=0,
    )


def factor_forms(unit_real, unit_imag):
    pairs = [
        kron_range(unit_real, unit_imag, 0, HALF),
        kron_range(unit_real, unit_imag, HALF, TRANSMONS),
    ]
    forward_left = [real_form(matrix_real, matrix_imag) for matrix_real, matrix_imag in pairs]
    forward_right = [real_form(matrix_real, -matrix_imag) for matrix_real, matrix_imag in pairs]
    adjoint_left = [real_form(matrix_real.T, -matrix_imag.T) for matrix_real, matrix_imag in pairs]
    adjoint_right = [real_form(matrix_real.T, matrix_imag.T) for matrix_real, matrix_imag in pairs]
    return (forward_left, forward_right, adjoint_left, adjoint_right)


def apply_factor(field, form, leading, trailing):
    width = form.shape[3]
    shaped = field.reshape(2, leading, width, trailing)
    result = jnp.einsum("cgdf,dpfq->cpgq", form, shaped, precision=TOP_ACCURACY)
    return result.reshape(field.shape)


def apply_factors(field, forms, leading, trailing):
    widths = [form.shape[3] for form in forms]
    for position, form in enumerate(forms):
        before = math.prod(widths[:position])
        after = math.prod(widths[position + 1 :])
        field = apply_factor(field, form, leading * before, after * trailing)
    return field


def step_unitaries(pulse, segment, clock, span, detuning):
    onehot = (jnp.arange(SEGMENTS, dtype=jnp.int32) == segment).astype(jnp.float32)
    theta = jnp.einsum("s,skm->km", onehot, pulse, precision=TOP_ACCURACY)
    multiple = jnp.arange(1, LEVELS, dtype=jnp.int32).astype(jnp.float32)
    phi = detuning[:, None] * (clock + 0.5 * span) * multiple[None, :]
    return rotations(theta, phi)


def sandwich(field, left_forms, right_forms):
    local_rows = field.shape[1]
    order_size = field.shape[2]
    members = lax.axis_size("row")
    block_width = order_size // members
    halfway = apply_factors(field, right_forms, local_rows, 1)
    halfway = halfway.reshape(2, local_rows, members, block_width)
    received = lax.all_to_all(halfway, "row", split_axis=2, concat_axis=1, tiled=True)
    count = received.shape[3]
    columns = apply_factors(received.reshape(2, order_size, count), left_forms, 1, count)
    turned = jnp.stack([columns[0].T, -columns[1].T])
    result = turned.reshape(2, 1, count, order_size)
    return result.reshape(2, block_width, order_size)


def local(linkage, pulse, segments, ticks, detuning, level_shift, coupling, dephase):
    current = linkage[:, 0]
    local_rows = current.shape[1]
    order_size = current.shape[2]
    row_rank = lax.axis_index("row")
    row_levels = digits(row_rank * local_rows + jnp.arange(local_rows, dtype=jnp.int32))
    col_levels = digits(jnp.arange(order_size, dtype=jnp.int32))
    decay, detune_grid = drift_tables(row_levels, col_levels, level_shift, coupling, dephase)
    step_ticks = ticks[0]

    def add_ticks(earlier, later):
        return earlier + later

    offsets = prefix(
        jnp.sum(step_ticks, keepdims=True, dtype=jnp.int32),
        "phase",
        add_ticks,
        jnp.zeros((1,), jnp.int32),
    )
    prepared = []
    for step_index in range(STEPS):
        span = step_ticks[step_index].astype(jnp.float32)
        clock = (offsets[0] + jnp.sum(step_ticks[:step_index], dtype=jnp.int32)).astype(jnp.float32)
        unit_real, unit_imag = step_unitaries(pulse, segments[0, step_index], clock, span, detuning)
        factor_real, factor_imag = half_factor(decay, detune_grid, span)
        prepared.append((factor_real, factor_imag, factor_forms(unit_real, unit_imag)))
    following = shifted(current, "phase", -1)
    field = current
    for forward_step_index in range(STEPS):
        forward_factor_real, forward_factor_imag, forward_forms = prepared[forward_step_index]
        field = weigh(field, forward_factor_real, forward_factor_imag)
        field = sandwich(field, forward_forms[0], forward_forms[1])
        field = weigh(field, forward_factor_real, forward_factor_imag)
    mismatch = field - following
    earlier_mismatch = shifted(mismatch, "phase", 1)
    adjoint = mismatch
    for step_index in reversed(range(STEPS)):
        factor_real, factor_imag, forms = prepared[step_index]
        adjoint = weigh(adjoint, factor_real, -factor_imag)
        adjoint = sandwich(adjoint, forms[2], forms[3])
        adjoint = weigh(adjoint, factor_real, -factor_imag)
    return (adjoint - earlier_mismatch)[:, None]


def table_slots():
    quads = STEPS * TRANSMONS * LEVELS * LEVELS
    names = [("q", quads), ("w", STEPS * TRANSMONS), ("t", STEPS), ("e", TRANSMONS)]
    names += [("c", TRANSMONS - 1), ("d", TRANSMONS)]
    slots, offset = {}, 0
    for name, count in names:
        slots[name] = offset
        offset += count
    return slots


def dot3(left_high, left_low, right_high, right_low, contract_right=0):
    dims = (((1,), (contract_right,)), ((), ()))

    def one(left, right):
        return lax.dot_general(left, right, dims, preferred_element_type=jnp.float32)

    return one(left_high, right_high) + (one(left_high, right_low) + one(left_low, right_high))


def split(value):
    high = value.astype(jnp.bfloat16)
    return high, (value - high.astype(jnp.float32)).astype(jnp.bfloat16)


def kernel(
    phases,
    members,
    scalars,
    state,
    out,
    following,
    mismatch,
    earlier,
    first_high,
    first_low,
    second_high,
    second_low,
    sides,
    pre_table,
    mid_table,
    post_table,
    turned,
    gathered_high,
    gathered_low,
    halfway,
    send_one,
    receive_one,
    send_two,
    receive_two,
    send_sems,
    receive_sems,
    phase_sems,
    own_sems,
):
    phase = lax.axis_index("phase")
    me = lax.axis_index("row")
    rows, order = state.shape[1], state.shape[2]
    lead = LEVELS**HALF
    trail = order // lead
    count = trail // members
    lanes = lead * count
    per = lead // members
    slots = table_slots()

    def q(step, k, i, j):
        return scalars[slots["q"] + ((step * TRANSMONS + k) * LEVELS + i) * LEVELS + j]

    def digit(index, k):
        return (index >> (2 * (TRANSMONS - 1 - k))) & (LEVELS - 1)

    barrier = pltpu.get_barrier_semaphore()
    after, before = lax.rem(phase + 1, phases), lax.rem(phase + phases - 1, phases)
    for offset in range(1, members):
        peer = lax.rem(me + offset, members)
        pl.semaphore_signal(barrier, inc=1, device_id=(phase, peer), device_id_type=MESH)
    for peer in (after, before):
        pl.semaphore_signal(barrier, inc=1, device_id=(peer, me), device_id_type=MESH)

    def pick(index, k, values):
        place = digit(index, k)
        result = jnp.where(place == 0, values[0], values[1])
        result = jnp.where(place == 2, values[2], result)
        return jnp.where(place == 3, values[3], result)

    def entries(row_index, col_index, k, step, swapped):
        vectors = []
        for i in range(LEVELS):
            values = [q(step, k, j, i) if swapped else q(step, k, i, j) for j in range(LEVELS)]
            vectors.append(pick(col_index, k, values))
        return pick(row_index, k, vectors)

    def kron_entries(row_index, col_index, ks, step, swapped):
        result = entries(row_index, col_index, ks[0], step, swapped)
        for k in ks[1:]:
            result = result * entries(row_index, col_index, k, step, swapped)
        return result

    head, tail = range(HALF), range(HALF, TRANSMONS)

    def iota(shape, axis):
        return lax.broadcasted_iota(jnp.int32, shape, axis)

    def build_dense(high, low, step, swapped):
        lane = iota((1, lanes), 1)
        lead_rows = [
            kron_entries(
                jnp.full((1, 1), a * trail, jnp.int32), (lane // count) * trail, head, step, swapped
            )
            for a in range(lead)
        ]
        for block in range(members):
            tile = kron_entries(
                iota((trail, 1), 0), block * count + lane % count, tail, step, swapped
            )
            for a in range(lead):
                upper, lower = split(tile * lead_rows[a])
                where = (slice(a * trail, (a + 1) * trail), slice(block * lanes, (block + 1) * lanes))
                high[where] = upper
                low[where] = lower

    def build_sides(step):
        row, col = iota((rows, 1), 0), iota((1, rows), 1)
        same = (row // trail) == (col // trail)
        lrow, lcol = iota((lanes, 1), 0), iota((1, lanes), 1)
        aligned = (lrow % count) == (lcol % count)
        for swapped in (False, True):
            body = kron_entries(row % trail, col % trail, tail, step, swapped)
            upper, lower = split(jnp.where(same, body, 0.0))
            base = 8 * step + 4 * swapped
            sides[base] = upper
            sides[base + 1] = lower
            body = kron_entries(
                (lrow // count) * trail, (lcol // count) * trail, head, step, swapped
            )
            upper, lower = split(jnp.where(aligned, body, 0.0))
            sides[base + 2] = upper
            sides[base + 3] = lower

    tau = [scalars[slots["t"] + s] for s in range(STEPS)]

    def angle(index, which):
        n = [digit(index, k).astype(jnp.float32) for k in range(TRANSMONS)]
        energy = jnp.zeros(index.shape, jnp.float32)
        for k in range(TRANSMONS):
            energy = energy + scalars[slots["e"] + k] * (n[k] * (n[k] - 1.0) * 0.5)
        for k in range(TRANSMONS - 1):
            energy = energy + scalars[slots["c"] + k] * (n[k] * n[k + 1])
        triangle = [v * (v + 1.0) * 0.5 for v in n]
        spin = [
            sum(scalars[slots["w"] + s * TRANSMONS + k] * triangle[k] for k in range(TRANSMONS))
            for s in range(STEPS)
        ]
        if which == 0:
            return -spin[0] - 0.5 * tau[0] * energy
        if which == 1:
            return (spin[0] - spin[1]) - 0.5 * (tau[0] + tau[1]) * energy
        return spin[1] - 0.5 * tau[1] * energy

    spans = (tau[0], tau[0] + tau[1], tau[1])

    def waves(index, which):
        value = angle(index, which)
        return jnp.cos(value), jnp.sin(value)

    def factor(row_index, col_index, row_waves, col_waves, which):
        decay = 0.0
        for k in range(TRANSMONS):
            gap = digit(row_index, k).astype(jnp.float32) - digit(col_index, k).astype(jnp.float32)
            decay = decay + scalars[slots["d"] + k] * (gap * gap)
        size = jnp.exp(-0.5 * spans[which] * decay)
        row_cos, row_sin = row_waves
        col_cos, col_sin = col_waves
        return (
            size * (row_cos * col_cos + row_sin * col_sin),
            size * (row_sin * col_cos - row_cos * col_sin),
        )

    width = 128

    def build_row_table(table, which):
        row = me * rows + iota((rows, 1), 0)
        row_waves = waves(row, which)
        for chunk in range(order // width):
            col = chunk * width + iota((1, width), 1)
            real, imag = factor(row, col, row_waves, waves(col, which), which)
            table[0, :, pl.ds(chunk * width, width)] = real
            table[1, :, pl.ds(chunk * width, width)] = imag

    def build_mid_table():
        for block in range(members):
            other = lax.rem(me + members - block, members)
            lrow, lane = iota((lanes, 1), 0), iota((1, lanes), 1)
            row = (lrow // count) * trail + block * count + lrow % count
            col = (lane // count) * trail + other * count + lane % count
            real, imag = factor(row, col, waves(row, 1), waves(col, 1), 1)
            mid_table[0, block] = real
            mid_table[1, block] = imag

    def exchange(source, target, trip):
        copies = []
        for offset in range(1, members):
            peer = lax.rem(me + offset, members)
            copy = pltpu.make_async_remote_copy(
                src_ref=source.at[peer],
                dst_ref=target.at[me],
                send_sem=send_sems.at[trip, offset],
                recv_sem=receive_sems.at[trip, offset],
                device_id=(phase, peer),
                device_id_type=MESH,
            )
            copy.start()
            copies.append(copy)
        own = pltpu.make_async_copy(source.at[me], target.at[me], own_sems.at[trip])
        own.start()
        copies.append(own)
        return copies

    def hand(source, target, peer, number):
        copy = pltpu.make_async_remote_copy(
            src_ref=source,
            dst_ref=target,
            send_sem=phase_sems.at[0, number],
            recv_sem=phase_sems.at[1, number],
            device_id=(peer, me),
            device_id_type=MESH,
        )
        copy.start()
        return copy

    def outbound(read, sign, table, side, high, low, trip):
        left_high, left_low = sides[side], sides[side + 1]
        for chunk in range(order // width):
            where = pl.ds(chunk * width, width)
            straight, crossed = read(where)
            value = table[0, :, where] * straight + sign * (table[1, :, where] * crossed)
            moved = dot3(left_high, left_low, *split(value))
            upper, lower = split(moved)
            gathered_high[0:rows, where] = upper
            gathered_low[0:rows, where] = lower
        pack = 2
        for pair in range(members // pack):
            where = pl.ds(pair * pack * lanes, pack * lanes)
            moved = dot3(
                gathered_high[0:rows, :], gathered_low[0:rows, :], high[:, where], low[:, where]
            )
            for inner in range(pack):
                block = pair * pack + inner
                for b in range(members):
                    for part in range(per):
                        start = part * trail + b * count
                        send_one[trip // 2, (b + block) % members, start : start + count, :] = moved[
                            start : start + count, inner * lanes : (inner + 1) * lanes
                        ]
        return exchange(send_one.at[trip // 2], receive_one.at[trip // 2], trip)

    def middle(sign, first_side, second_side, trip):
        went = trip // 2
        for block in range(members):
            pieces = []
            for a in range(lead):
                start = (a % per) * trail + block * count
                pieces.append(receive_one[went, a // per, start : start + count, :])
            value = jnp.concatenate(pieces, axis=0)
            turned[block] = dot3(sides[first_side], sides[first_side + 1], *split(value))
        for block in range(members):
            other = lax.rem(me + members - block, members)
            straight = turned[block]
            crossed = turned[other].T
            real, imag = mid_table[0, block], sign * mid_table[1, block]
            for kind, value in enumerate(
                (real * straight + imag * crossed, real * crossed - imag * straight)
            ):
                moved = dot3(sides[second_side], sides[second_side + 1], *split(value))
                for a in range(lead):
                    start = (a % per) * trail + block * count
                    send_two[went, a // per, kind, start : start + count, :] = moved[
                        a * count : (a + 1) * count, :
                    ]
        return exchange(send_two.at[went], receive_two.at[went], trip)

    def inbound(side, high, low, trip):
        went = trip // 2
        for block in range(members):
            for kind in range(2):
                pieces = []
                for part in range(per):
                    for b in range(members):
                        start = part * trail + b * count
                        pieces.append(
                            receive_two[went, (b + block) % members, kind, start : start + count, :]
                        )
                upper, lower = split(jnp.concatenate(pieces, axis=0))
                where = (slice(kind * rows, (kind + 1) * rows), slice(block * lanes, (block + 1) * lanes))
                gathered_high[where] = upper
                gathered_low[where] = lower
        wide = 2 * width
        for chunk in range(order // wide):
            where = pl.ds(chunk * wide, wide)
            moved = dot3(gathered_high[...], gathered_low[...], high[where, :], low[where, :], 1)
            for kind in range(2):
                halfway[kind, :, where] = dot3(
                    sides[side], sides[side + 1], *split(moved[kind * rows : (kind + 1) * rows])
                )

    def wait(copies):
        for copy in copies:
            copy.wait()

    build_row_table(pre_table, 0)
    build_dense(first_high, first_low, 0, True)
    build_sides(0)
    pl.semaphore_wait(barrier, members + 1)

    def read_state(where):
        real, imag = state[0, :, where], state[1, :, where]
        return real + imag, real - imag

    copies = outbound(read_state, 1.0, pre_table, 0, first_high, first_low, 0)
    handed = hand(state, following, before, 0)
    build_sides(1)
    build_mid_table()
    build_dense(second_high, second_low, 1, False)
    build_row_table(post_table, 2)
    wait(copies)
    copies = middle(1.0, 2, 10, 1)
    handed.wait()
    wait(copies)
    inbound(8, second_high, second_low, 1)
    for chunk in range(order // width):
        where = pl.ds(chunk * width, width)
        straight, crossed = halfway[0, :, where], halfway[1, :, where]
        real, imag = post_table[0, :, where], post_table[1, :, where]
        next_real, next_imag = following[0, :, where], following[1, :, where]
        mismatch[0, :, where] = real * straight + imag * crossed - (next_real + next_imag)
        mismatch[1, :, where] = real * crossed - imag * straight - (next_real - next_imag)

    def read_mismatch(where):
        return mismatch[0, :, where], mismatch[1, :, where]

    copies = outbound(read_mismatch, -1.0, post_table, 12, second_high, second_low, 2)
    handed = hand(mismatch, earlier, after, 1)
    wait(copies)
    copies = middle(-1.0, 14, 6, 3)
    handed.wait()
    wait(copies)
    inbound(4, first_high, first_low, 3)
    for chunk in range(order // width):
        where = pl.ds(chunk * width, width)
        straight, crossed = halfway[0, :, where], halfway[1, :, where]
        real, imag = pre_table[0, :, where], -pre_table[1, :, where]
        upper = real * straight + imag * crossed - earlier[0, :, where]
        lower = real * crossed - imag * straight - earlier[1, :, where]
        out[0, :, where] = 0.5 * (upper + lower)
        out[1, :, where] = 0.5 * (upper - lower)


def fused(linkage, pulse, segments, ticks, detuning, level_shift, coupling, dephase):
    phases, members = lax.axis_size("phase"), lax.axis_size("row")
    current = linkage[:, 0]
    rows, order = current.shape[1], current.shape[2]
    mine = lax.axis_index("phase")
    total = jnp.sum(ticks, axis=1, dtype=jnp.int32)
    start = jnp.zeros((1,), jnp.int32)
    for distance in range(1, phases):
        other = shifted(total, "phase", distance)
        start = start + jnp.where(mine >= distance, other, 0)
    tau = ticks[0].astype(jnp.float32)
    clock = (start + jnp.cumsum(ticks[0]) - ticks[0]).astype(jnp.float32)
    spin = (clock + 0.5 * tau)[:, None] * detuning[None, :]
    onehot = (segments[0][:, None] == jnp.arange(SEGMENTS, dtype=jnp.int32)[None, :])
    theta = jnp.sum(jnp.where(onehot[:, :, None, None], pulse[None], 0.0), axis=1)
    cosine, sine = jnp.cos(theta), jnp.sin(theta)
    one = jnp.ones_like(cosine[:, :, 0])
    cells = []
    for i in range(LEVELS):
        for j in range(LEVELS):
            if i > j + 1:
                cells.append(0.0 * one)
            elif i == j + 1:
                cells.append(sine[:, :, j])
            else:
                cell = one if i == 0 else cosine[:, :, i - 1]
                for m in range(i, j):
                    cell = cell * -sine[:, :, m]
                cells.append(cell if j == LEVELS - 1 else cell * cosine[:, :, j])
    quads = jnp.stack(cells, axis=-1)
    scalars = jnp.concatenate(
        [quads.reshape(-1), spin.reshape(-1), tau, level_shift, coupling, dephase]
    )
    lanes = order // members
    full = (2, rows, order)
    one_way = (2, members, rows, lanes)
    two_way = (2, members, 2, rows, lanes)
    vmem = pl.BlockSpec(memory_space=pltpu.VMEM)
    result = pl.pallas_call(
        functools.partial(kernel, phases, members),
        out_shape=jax.ShapeDtypeStruct(full, jnp.float32),
        in_specs=[pl.BlockSpec(memory_space=pltpu.SMEM), vmem],
        out_specs=vmem,
        scratch_shapes=[
            pltpu.VMEM(full, jnp.float32),
            pltpu.VMEM(full, jnp.float32),
            pltpu.VMEM(full, jnp.float32),
            pltpu.VMEM((order, order), jnp.bfloat16),
            pltpu.VMEM((order, order), jnp.bfloat16),
            pltpu.VMEM((order, order), jnp.bfloat16),
            pltpu.VMEM((order, order), jnp.bfloat16),
            pltpu.VMEM((8 * STEPS, rows, rows), jnp.bfloat16),
            pltpu.VMEM(full, jnp.float32),
            pltpu.VMEM((2, members, lanes, lanes), jnp.float32),
            pltpu.VMEM(full, jnp.float32),
            pltpu.VMEM((members, lanes, lanes), jnp.float32),
            pltpu.VMEM((2 * rows, order), jnp.bfloat16),
            pltpu.VMEM((2 * rows, order), jnp.bfloat16),
            pltpu.VMEM(full, jnp.float32),
            pltpu.VMEM(one_way, jnp.float32),
            pltpu.VMEM(one_way, jnp.float32),
            pltpu.VMEM(two_way, jnp.float32),
            pltpu.VMEM(two_way, jnp.float32),
            pltpu.SemaphoreType.DMA((4, members)),
            pltpu.SemaphoreType.DMA((4, members)),
            pltpu.SemaphoreType.DMA((2, 2)),
            pltpu.SemaphoreType.DMA((4,)),
        ],
        compiler_params=pltpu.CompilerParams(
            collective_id=0, has_side_effects=True, vmem_limit_bytes=56 * 1024 * 1024
        ),
    )(scalars, current)
    return result[:, None]


def solution(mesh):
    members = mesh.shape["row"]
    trail = LEVELS ** (TRANSMONS - HALF)
    fits = STEPS == 2 and members <= LEVELS**HALF and LEVELS**HALF * (trail // members) == 128
    return jax.shard_map(
        fused if fits else local,
        mesh=mesh,
        in_specs=(
            P(None, "phase", "row", None),
            P(),
            P("phase", None),
            P("phase", None),
            P(),
            P(),
            P(),
            P(),
        ),
        out_specs=P(None, "phase", "row", None),
        check_vma=False,
    )
```

```python
import functools
import math

import jax
import jax.numpy as jnp
from jax import lax
from jax.experimental import pallas as pl
from jax.experimental.pallas import tpu as pltpu
from jax.sharding import PartitionSpec as P

TRANSMONS = 5
LEVELS = 4
STEPS = 2
SEGMENTS = 32
HALF = 2
MESH = pl.DeviceIdType.MESH


TOP_ACCURACY = lax.Precision.HIGHEST


def prefix(value, axis, join, neutral):
    count, mine = (lax.axis_size(axis), lax.axis_index(axis))
    pieces = lax.all_gather(value, axis)
    subtotal = jnp.full_like(value, 0) + jnp.asarray(neutral, value.dtype)

    def lap(position, subtotal):
        longer = join(subtotal, pieces[position])
        return jnp.where(position < mine, longer, subtotal)

    return lax.fori_loop(0, count - 1, lap, subtotal)


def shifted(block, axis, distance):
    devices = range(lax.axis_size(axis))
    route = [((i - distance) % len(devices), i) for i in devices]
    return lax.ppermute(block, axis, route)


def digits(indices):
    powers = LEVELS ** (TRANSMONS - 1 - jnp.arange(TRANSMONS, dtype=jnp.int32))
    return (indices[None, :] // powers[:, None] % LEVELS).astype(jnp.float32)


def energies(levels, level_shift, coupling):
    own_part = jnp.sum(level_shift[:, None] * levels * (levels - 1.0) * 0.5, axis=0)
    return own_part + jnp.sum(coupling[:, None] * levels[:-1] * levels[1:], axis=0)


def drift_tables(row_levels, col_levels, level_shift, coupling, dephase):
    detune_grid = (
        energies(row_levels, level_shift, coupling)[:, None]
        - energies(col_levels, level_shift, coupling)[None, :]
    )
    weighted = dephase[:, None] * row_levels
    cross = jnp.dot(
        weighted.T, col_levels, preferred_element_type=jnp.float32, precision=TOP_ACCURACY
    )
    row_part = jnp.sum(weighted * row_levels, axis=0)
    col_part = jnp.sum(dephase[:, None] * col_levels * col_levels, axis=0)
    decay = row_part[:, None] + col_part[None, :] - 2.0 * cross
    return (decay, detune_grid)


def half_factor(decay, detune_grid, span):
    magnitude = jnp.exp(-0.5 * span * decay)
    return (
        magnitude * jnp.cos(0.5 * span * detune_grid),
        -magnitude * jnp.sin(0.5 * span * detune_grid),
    )


def weigh(field, factor_real, factor_imag):
    return jnp.stack(
        [
            field[0] * factor_real - field[1] * factor_imag,
            field[0] * factor_imag + field[1] * factor_real,
        ]
    )


def complex_product(left_real_component, left_imaginary, right_real_component, right_imaginary):
    real_component = jnp.einsum(
        "nmx,nxw->nmw", left_real_component, right_real_component, precision=TOP_ACCURACY
    ) - jnp.einsum("nmx,nxw->nmw", left_imaginary, right_imaginary, precision=TOP_ACCURACY)
    imaginary_component = jnp.einsum(
        "nmx,nxw->nmw", left_real_component, right_imaginary, precision=TOP_ACCURACY
    ) + jnp.einsum("nmx,nxw->nmw", left_imaginary, right_real_component, precision=TOP_ACCURACY)
    return (real_component, imaginary_component)


def rotations(theta, phi):
    identity = jnp.eye(LEVELS, dtype=jnp.float32)
    total_real = jnp.broadcast_to(identity, (theta.shape[0], LEVELS, LEVELS))
    total_imag = jnp.zeros((theta.shape[0], LEVELS, LEVELS), jnp.float32)
    for level in range(LEVELS - 1):
        upper = jnp.outer(identity[level], identity[level + 1])
        lower = upper.T
        block = jnp.outer(identity[level], identity[level]) + jnp.outer(
            identity[level + 1], identity[level + 1]
        )
        cosine = jnp.cos(theta[:, level])[:, None, None]
        sine = jnp.sin(theta[:, level])[:, None, None]
        phase_cos = jnp.cos(phi[:, level])[:, None, None]
        phase_sin = jnp.sin(phi[:, level])[:, None, None]
        rot_real = identity + (cosine - 1.0) * block + sine * phase_cos * (lower - upper)
        rot_imag = sine * phase_sin * (upper + lower)
        total_real, total_imag = complex_product(total_real, total_imag, rot_real, rot_imag)
    return (total_real, total_imag)


def kron_range(unit_real, unit_imag, first, last):
    acc_real, acc_imag = (unit_real[first], unit_imag[first])
    for transmon in range(first + 1, last):
        next_real, next_imag = (unit_real[transmon], unit_imag[transmon])
        acc_real, acc_imag = (
            jnp.kron(acc_real, next_real) - jnp.kron(acc_imag, next_imag),
            jnp.kron(acc_real, next_imag) + jnp.kron(acc_imag, next_real),
        )
    return (acc_real, acc_imag)


def real_form(matrix_real, matrix_imag):
    return jnp.stack(
        [
            jnp.stack([matrix_real, -matrix_imag], axis=1),
            jnp.stack([matrix_imag, matrix_real], axis=1),
        ],
        axis=0,
    )


def factor_forms(unit_real, unit_imag):
    pairs = [
        kron_range(unit_real, unit_imag, 0, HALF),
        kron_range(unit_real, unit_imag, HALF, TRANSMONS),
    ]
    forward_left = [real_form(matrix_real, matrix_imag) for matrix_real, matrix_imag in pairs]
    forward_right = [real_form(matrix_real, -matrix_imag) for matrix_real, matrix_imag in pairs]
    adjoint_left = [real_form(matrix_real.T, -matrix_imag.T) for matrix_real, matrix_imag in pairs]
    adjoint_right = [real_form(matrix_real.T, matrix_imag.T) for matrix_real, matrix_imag in pairs]
    return (forward_left, forward_right, adjoint_left, adjoint_right)


def apply_factor(field, form, leading, trailing):
    width = form.shape[3]
    shaped = field.reshape(2, leading, width, trailing)
    result = jnp.einsum("cgdf,dpfq->cpgq", form, shaped, precision=TOP_ACCURACY)
    return result.reshape(field.shape)


def apply_factors(field, forms, leading, trailing):
    widths = [form.shape[3] for form in forms]
    for position, form in enumerate(forms):
        before = math.prod(widths[:position])
        after = math.prod(widths[position + 1 :])
        field = apply_factor(field, form, leading * before, after * trailing)
    return field


def step_unitaries(pulse, segment, clock, span, detuning):
    onehot = (jnp.arange(SEGMENTS, dtype=jnp.int32) == segment).astype(jnp.float32)
    theta = jnp.einsum("s,skm->km", onehot, pulse, precision=TOP_ACCURACY)
    multiple = jnp.arange(1, LEVELS, dtype=jnp.int32).astype(jnp.float32)
    phi = detuning[:, None] * (clock + 0.5 * span) * multiple[None, :]
    return rotations(theta, phi)


def sandwich(field, left_forms, right_forms):
    local_rows = field.shape[1]
    order_size = field.shape[2]
    members = lax.axis_size("row")
    block_width = order_size // members
    halfway = apply_factors(field, right_forms, local_rows, 1)
    halfway = halfway.reshape(2, local_rows, members, block_width)
    received = lax.all_to_all(halfway, "row", split_axis=2, concat_axis=1, tiled=True)
    count = received.shape[3]
    columns = apply_factors(received.reshape(2, order_size, count), left_forms, 1, count)
    turned = jnp.stack([columns[0].T, -columns[1].T])
    result = turned.reshape(2, 1, count, order_size)
    return result.reshape(2, block_width, order_size)


def local(linkage, pulse, segments, ticks, detuning, level_shift, coupling, dephase):
    current = linkage[:, 0]
    local_rows = current.shape[1]
    order_size = current.shape[2]
    row_rank = lax.axis_index("row")
    row_levels = digits(row_rank * local_rows + jnp.arange(local_rows, dtype=jnp.int32))
    col_levels = digits(jnp.arange(order_size, dtype=jnp.int32))
    decay, detune_grid = drift_tables(row_levels, col_levels, level_shift, coupling, dephase)
    step_ticks = ticks[0]

    def add_ticks(earlier, later):
        return earlier + later

    offsets = prefix(
        jnp.sum(step_ticks, keepdims=True, dtype=jnp.int32),
        "phase",
        add_ticks,
        jnp.zeros((1,), jnp.int32),
    )
    prepared = []
    for step_index in range(STEPS):
        span = step_ticks[step_index].astype(jnp.float32)
        clock = (offsets[0] + jnp.sum(step_ticks[:step_index], dtype=jnp.int32)).astype(jnp.float32)
        unit_real, unit_imag = step_unitaries(pulse, segments[0, step_index], clock, span, detuning)
        factor_real, factor_imag = half_factor(decay, detune_grid, span)
        prepared.append((factor_real, factor_imag, factor_forms(unit_real, unit_imag)))
    following = shifted(current, "phase", -1)
    field = current
    for forward_step_index in range(STEPS):
        forward_factor_real, forward_factor_imag, forward_forms = prepared[forward_step_index]
        field = weigh(field, forward_factor_real, forward_factor_imag)
        field = sandwich(field, forward_forms[0], forward_forms[1])
        field = weigh(field, forward_factor_real, forward_factor_imag)
    mismatch = field - following
    earlier_mismatch = shifted(mismatch, "phase", 1)
    adjoint = mismatch
    for step_index in reversed(range(STEPS)):
        factor_real, factor_imag, forms = prepared[step_index]
        adjoint = weigh(adjoint, factor_real, -factor_imag)
        adjoint = sandwich(adjoint, forms[2], forms[3])
        adjoint = weigh(adjoint, factor_real, -factor_imag)
    return (adjoint - earlier_mismatch)[:, None]


def dot3(left_high, left_low, right_high, right_low, contract_right=0):
    dims = (((1,), (contract_right,)), ((), ()))

    def one(left, right):
        return lax.dot_general(left, right, dims, preferred_element_type=jnp.float32)

    return one(left_high, right_high) + (one(left_high, right_low) + one(left_low, right_high))


def split(value):
    high = value.astype(jnp.bfloat16)
    return high, (value - high.astype(jnp.float32)).astype(jnp.bfloat16)


def rotation_cells(cosine, sine, k):
    def at(table, m):
        return table[k : k + 1, m : m + 1]

    rows = []
    for i in range(LEVELS):
        row = []
        for j in range(LEVELS):
            if i > j + 1:
                row.append(jnp.zeros((1, 1), jnp.float32))
            elif i == j + 1:
                row.append(at(sine, j))
            else:
                factors = [] if i == 0 else [at(cosine, i - 1)]
                factors += [-at(sine, m) for m in range(i, j)]
                factors += [] if j == LEVELS - 1 else [at(cosine, j)]
                row.append(math.prod(factors[1:], start=factors[0]))
        rows.append(row)
    return rows


def kernel(
    phases,
    members,
    ticks,
    segments,
    detuning,
    level_shift,
    coupling,
    dephase,
    tick_row,
    pulse,
    state,
    out,
    tick_rows,
    following,
    mismatch,
    earlier,
    first_high,
    first_low,
    second_high,
    second_low,
    sides,
    pre_table,
    mid_table,
    post_table,
    turned,
    gathered_high,
    gathered_low,
    halfway,
    send_one,
    receive_one,
    send_two,
    receive_two,
    send_sems,
    receive_sems,
    phase_sems,
    own_sems,
    tick_sems,
):
    phase = lax.axis_index("phase")
    me = lax.axis_index("row")
    rows, order = state.shape[1], state.shape[2]
    lead = LEVELS**HALF
    trail = order // lead
    count = trail // members
    lanes = lead * count
    per = lead // members
    cells = []
    for step in range(STEPS):
        theta = pulse[segments[0, step]]
        cosine, sine = jnp.cos(theta), jnp.sin(theta)
        cells.append([rotation_cells(cosine, sine, k) for k in range(TRANSMONS)])

    def q(step, k, i, j):
        return cells[step][k][i][j]

    def digit(index, k):
        return (index >> (2 * (TRANSMONS - 1 - k))) & (LEVELS - 1)

    barrier = pltpu.get_barrier_semaphore()
    after, before = lax.rem(phase + 1, phases), lax.rem(phase + phases - 1, phases)
    for offset in range(1, members):
        peer = lax.rem(me + offset, members)
        pl.semaphore_signal(barrier, inc=1, device_id=(phase, peer), device_id_type=MESH)
    for distance in range(1, phases):
        peer = lax.rem(phase + distance, phases)
        pl.semaphore_signal(barrier, inc=1, device_id=(peer, me), device_id_type=MESH)

    def pick(index, k, values):
        place = digit(index, k)
        result = jnp.where(place == 0, values[0], values[1])
        result = jnp.where(place == 2, values[2], result)
        return jnp.where(place == 3, values[3], result)

    def entries(row_index, col_index, k, step, swapped):
        vectors = []
        for i in range(LEVELS):
            values = [q(step, k, j, i) if swapped else q(step, k, i, j) for j in range(LEVELS)]
            vectors.append(pick(col_index, k, values))
        return pick(row_index, k, vectors)

    def kron_entries(row_index, col_index, ks, step, swapped):
        result = entries(row_index, col_index, ks[0], step, swapped)
        for k in ks[1:]:
            result = result * entries(row_index, col_index, k, step, swapped)
        return result

    head, tail = range(HALF), range(HALF, TRANSMONS)

    def iota(shape, axis):
        return lax.broadcasted_iota(jnp.int32, shape, axis)

    def build_dense(high, low, step, swapped):
        lane = iota((1, lanes), 1)
        lead_rows = [
            kron_entries(
                jnp.full((1, 1), a * trail, jnp.int32), (lane // count) * trail, head, step, swapped
            )
            for a in range(lead)
        ]
        for block in range(members):
            tile = kron_entries(
                iota((trail, 1), 0), block * count + lane % count, tail, step, swapped
            )
            for a in range(lead):
                upper, lower = split(tile * lead_rows[a])
                where = (slice(a * trail, (a + 1) * trail), slice(block * lanes, (block + 1) * lanes))
                high[where] = upper
                low[where] = lower

    def build_sides(step):
        row, col = iota((rows, 1), 0), iota((1, rows), 1)
        same = (row // trail) == (col // trail)
        lrow, lcol = iota((lanes, 1), 0), iota((1, lanes), 1)
        aligned = (lrow % count) == (lcol % count)
        for swapped in (False, True):
            body = kron_entries(row % trail, col % trail, tail, step, swapped)
            upper, lower = split(jnp.where(same, body, 0.0))
            base = 8 * step + 4 * swapped
            sides[base] = upper
            sides[base + 1] = lower
            body = kron_entries(
                (lrow // count) * trail, (lcol // count) * trail, head, step, swapped
            )
            upper, lower = split(jnp.where(aligned, body, 0.0))
            sides[base + 2] = upper
            sides[base + 3] = lower

    tau = [ticks[0, s].astype(jnp.float32) for s in range(STEPS)]

    def send_ticks():
        copies = []
        for distance in range(1, phases):
            copy = pltpu.make_async_remote_copy(
                src_ref=tick_row,
                dst_ref=tick_rows.at[phase],
                send_sem=tick_sems.at[0, distance],
                recv_sem=tick_sems.at[1, distance],
                device_id=(lax.rem(phase + distance, phases), me),
                device_id_type=MESH,
            )
            copy.start()
            copies.append(copy)
        return copies

    weights = []

    def set_weights():
        start = jnp.zeros((1, 1), jnp.int32)
        for distance in range(1, phases):
            row = tick_rows[lax.rem(phase + phases - distance, phases)]
            total = sum(row[:, s : s + 1] for s in range(STEPS))
            start = start + jnp.where(phase >= distance, total, 0)
        for s in range(STEPS):
            clock = start.astype(jnp.float32)
            weights.append([(clock + 0.5 * tau[s]) * detuning[k] for k in range(TRANSMONS)])
            start = start + ticks[0, s]

    def angle(index, which):
        n = [digit(index, k).astype(jnp.float32) for k in range(TRANSMONS)]
        energy = jnp.zeros(index.shape, jnp.float32)
        for k in range(TRANSMONS):
            energy = energy + level_shift[k] * (n[k] * (n[k] - 1.0) * 0.5)
        for k in range(TRANSMONS - 1):
            energy = energy + coupling[k] * (n[k] * n[k + 1])
        triangle = [v * (v + 1.0) * 0.5 for v in n]
        spin = [
            sum(weights[s][k] * triangle[k] for k in range(TRANSMONS))
            for s in range(STEPS)
        ]
        if which == 0:
            return -spin[0] - 0.5 * tau[0] * energy
        if which == 1:
            return (spin[0] - spin[1]) - 0.5 * (tau[0] + tau[1]) * energy
        return spin[1] - 0.5 * tau[1] * energy

    spans = (tau[0], tau[0] + tau[1], tau[1])

    def waves(index, which):
        value = angle(index, which)
        return jnp.cos(value), jnp.sin(value)

    def factor(row_index, col_index, row_waves, col_waves, which):
        decay = 0.0
        for k in range(TRANSMONS):
            gap = digit(row_index, k).astype(jnp.float32) - digit(col_index, k).astype(jnp.float32)
            decay = decay + dephase[k] * (gap * gap)
        size = jnp.exp(-0.5 * spans[which] * decay)
        row_cos, row_sin = row_waves
        col_cos, col_sin = col_waves
        return (
            size * (row_cos * col_cos + row_sin * col_sin),
            size * (row_sin * col_cos - row_cos * col_sin),
        )

    width = 128

    def build_row_table(table, which):
        row = me * rows + iota((rows, 1), 0)
        row_waves = waves(row, which)
        for chunk in range(order // width):
            col = chunk * width + iota((1, width), 1)
            real, imag = factor(row, col, row_waves, waves(col, which), which)
            table[0, :, pl.ds(chunk * width, width)] = real
            table[1, :, pl.ds(chunk * width, width)] = imag

    def build_mid_table():
        for block in range(members):
            other = lax.rem(me + members - block, members)
            lrow, lane = iota((lanes, 1), 0), iota((1, lanes), 1)
            row = (lrow // count) * trail + block * count + lrow % count
            col = (lane // count) * trail + other * count + lane % count
            real, imag = factor(row, col, waves(row, 1), waves(col, 1), 1)
            mid_table[0, block] = real
            mid_table[1, block] = imag

    def exchange(source, target, trip):
        copies = []
        for offset in range(1, members):
            peer = lax.rem(me + offset, members)
            copy = pltpu.make_async_remote_copy(
                src_ref=source.at[peer],
                dst_ref=target.at[me],
                send_sem=send_sems.at[trip, offset],
                recv_sem=receive_sems.at[trip, offset],
                device_id=(phase, peer),
                device_id_type=MESH,
            )
            copy.start()
            copies.append(copy)
        own = pltpu.make_async_copy(source.at[me], target.at[me], own_sems.at[trip])
        own.start()
        copies.append(own)
        return copies

    def hand(source, target, peer, number):
        copy = pltpu.make_async_remote_copy(
            src_ref=source,
            dst_ref=target,
            send_sem=phase_sems.at[0, number],
            recv_sem=phase_sems.at[1, number],
            device_id=(peer, me),
            device_id_type=MESH,
        )
        copy.start()
        return copy

    def outbound(read, sign, table, side, high, low, trip):
        left_high, left_low = sides[side], sides[side + 1]
        for chunk in range(order // width):
            where = pl.ds(chunk * width, width)
            straight, crossed = read(where)
            value = table[0, :, where] * straight + sign * (table[1, :, where] * crossed)
            moved = dot3(left_high, left_low, *split(value))
            upper, lower = split(moved)
            gathered_high[0:rows, where] = upper
            gathered_low[0:rows, where] = lower
        pack = 2
        for pair in range(members // pack):
            where = pl.ds(pair * pack * lanes, pack * lanes)
            moved = dot3(
                gathered_high[0:rows, :], gathered_low[0:rows, :], high[:, where], low[:, where]
            )
            for inner in range(pack):
                block = pair * pack + inner
                for b in range(members):
                    for part in range(per):
                        start = part * trail + b * count
                        send_one[trip // 2, (b + block) % members, start : start + count, :] = moved[
                            start : start + count, inner * lanes : (inner + 1) * lanes
                        ]
        return exchange(send_one.at[trip // 2], receive_one.at[trip // 2], trip)

    def middle(sign, first_side, second_side, trip):
        went = trip // 2
        for block in range(members):
            pieces = []
            for a in range(lead):
                start = (a % per) * trail + block * count
                pieces.append(receive_one[went, a // per, start : start + count, :])
            value = jnp.concatenate(pieces, axis=0)
            turned[block] = dot3(sides[first_side], sides[first_side + 1], *split(value))
        for block in range(members):
            other = lax.rem(me + members - block, members)
            straight = turned[block]
            crossed = turned[other].T
            real, imag = mid_table[0, block], sign * mid_table[1, block]
            for kind, value in enumerate(
                (real * straight + imag * crossed, real * crossed - imag * straight)
            ):
                moved = dot3(sides[second_side], sides[second_side + 1], *split(value))
                for a in range(lead):
                    start = (a % per) * trail + block * count
                    send_two[went, a // per, kind, start : start + count, :] = moved[
                        a * count : (a + 1) * count, :
                    ]
        return exchange(send_two.at[went], receive_two.at[went], trip)

    def inbound(side, high, low, trip):
        went = trip // 2
        for block in range(members):
            for kind in range(2):
                pieces = []
                for part in range(per):
                    for b in range(members):
                        start = part * trail + b * count
                        pieces.append(
                            receive_two[went, (b + block) % members, kind, start : start + count, :]
                        )
                upper, lower = split(jnp.concatenate(pieces, axis=0))
                where = (slice(kind * rows, (kind + 1) * rows), slice(block * lanes, (block + 1) * lanes))
                gathered_high[where] = upper
                gathered_low[where] = lower
        wide = 2 * width
        for chunk in range(order // wide):
            where = pl.ds(chunk * wide, wide)
            moved = dot3(gathered_high[...], gathered_low[...], high[where, :], low[where, :], 1)
            for kind in range(2):
                halfway[kind, :, where] = dot3(
                    sides[side], sides[side + 1], *split(moved[kind * rows : (kind + 1) * rows])
                )

    def wait(copies):
        for copy in copies:
            copy.wait()

    pl.semaphore_wait(barrier, members + phases - 2)
    tick_copies = send_ticks()
    handed = hand(state, following, before, 0)
    build_dense(first_high, first_low, 0, True)
    build_sides(0)
    for copy in tick_copies:
        copy.wait()
    set_weights()
    build_row_table(pre_table, 0)

    def read_state(where):
        real, imag = state[0, :, where], state[1, :, where]
        return real + imag, real - imag

    copies = outbound(read_state, 1.0, pre_table, 0, first_high, first_low, 0)
    build_sides(1)
    build_mid_table()
    build_dense(second_high, second_low, 1, False)
    build_row_table(post_table, 2)
    wait(copies)
    copies = middle(1.0, 2, 10, 1)
    handed.wait()
    wait(copies)
    inbound(8, second_high, second_low, 1)
    for chunk in range(order // width):
        where = pl.ds(chunk * width, width)
        straight, crossed = halfway[0, :, where], halfway[1, :, where]
        real, imag = post_table[0, :, where], post_table[1, :, where]
        next_real, next_imag = following[0, :, where], following[1, :, where]
        mismatch[0, :, where] = real * straight + imag * crossed - (next_real + next_imag)
        mismatch[1, :, where] = real * crossed - imag * straight - (next_real - next_imag)

    def read_mismatch(where):
        return mismatch[0, :, where], mismatch[1, :, where]

    copies = outbound(read_mismatch, -1.0, post_table, 12, second_high, second_low, 2)
    handed = hand(mismatch, earlier, after, 1)
    wait(copies)
    copies = middle(-1.0, 14, 6, 3)
    handed.wait()
    wait(copies)
    inbound(4, first_high, first_low, 3)
    for chunk in range(order // width):
        where = pl.ds(chunk * width, width)
        straight, crossed = halfway[0, :, where], halfway[1, :, where]
        real, imag = pre_table[0, :, where], -pre_table[1, :, where]
        upper = real * straight + imag * crossed - earlier[0, :, where]
        lower = real * crossed - imag * straight - earlier[1, :, where]
        out[0, :, where] = 0.5 * (upper + lower)
        out[1, :, where] = 0.5 * (upper - lower)


def fused(linkage, pulse, segments, ticks, detuning, level_shift, coupling, dephase):
    phases, members = lax.axis_size("phase"), lax.axis_size("row")
    current = linkage[:, 0]
    rows, order = current.shape[1], current.shape[2]
    lanes = order // members
    full = (2, rows, order)
    one_way = (2, members, rows, lanes)
    two_way = (2, members, 2, rows, lanes)
    vmem = pl.BlockSpec(memory_space=pltpu.VMEM)
    result = pl.pallas_call(
        functools.partial(kernel, phases, members),
        out_shape=jax.ShapeDtypeStruct(full, jnp.float32),
        in_specs=[pl.BlockSpec(memory_space=pltpu.SMEM)] * 6 + [vmem] * 3,
        out_specs=vmem,
        scratch_shapes=[
            pltpu.VMEM((phases, 1, STEPS), jnp.int32),
            pltpu.VMEM(full, jnp.float32),
            pltpu.VMEM(full, jnp.float32),
            pltpu.VMEM(full, jnp.float32),
            pltpu.VMEM((order, order), jnp.bfloat16),
            pltpu.VMEM((order, order), jnp.bfloat16),
            pltpu.VMEM((order, order), jnp.bfloat16),
            pltpu.VMEM((order, order), jnp.bfloat16),
            pltpu.VMEM((8 * STEPS, rows, rows), jnp.bfloat16),
            pltpu.VMEM(full, jnp.float32),
            pltpu.VMEM((2, members, lanes, lanes), jnp.float32),
            pltpu.VMEM(full, jnp.float32),
            pltpu.VMEM((members, lanes, lanes), jnp.float32),
            pltpu.VMEM((2 * rows, order), jnp.bfloat16),
            pltpu.VMEM((2 * rows, order), jnp.bfloat16),
            pltpu.VMEM(full, jnp.float32),
            pltpu.VMEM(one_way, jnp.float32),
            pltpu.VMEM(one_way, jnp.float32),
            pltpu.VMEM(two_way, jnp.float32),
            pltpu.VMEM(two_way, jnp.float32),
            pltpu.SemaphoreType.DMA((4, members)),
            pltpu.SemaphoreType.DMA((4, members)),
            pltpu.SemaphoreType.DMA((2, 2)),
            pltpu.SemaphoreType.DMA((4,)),
            pltpu.SemaphoreType.DMA((2, phases)),
        ],
        compiler_params=pltpu.CompilerParams(
            collective_id=0, has_side_effects=True, vmem_limit_bytes=56 * 1024 * 1024
        ),
    )(ticks, segments, detuning, level_shift, coupling, dephase, ticks, pulse, current)
    return result[:, None]


def solution(mesh):
    members = mesh.shape["row"]
    trail = LEVELS ** (TRANSMONS - HALF)
    fits = STEPS == 2 and members <= LEVELS**HALF and LEVELS**HALF * (trail // members) == 128
    return jax.shard_map(
        fused if fits else local,
        mesh=mesh,
        in_specs=(
            P(None, "phase", "row", None),
            P(),
            P("phase", None),
            P("phase", None),
            P(),
            P(),
            P(),
            P(),
        ),
        out_specs=P(None, "phase", "row", None),
        check_vma=False,
    )
```

```python
import functools
import math

import jax
import jax.numpy as jnp
from jax import lax
from jax.experimental import pallas as pl
from jax.experimental.pallas import tpu as pltpu
from jax.sharding import PartitionSpec as P

TRANSMONS = 5
LEVELS = 4
STEPS = 2
SEGMENTS = 32
HALF = 2
MESH = pl.DeviceIdType.MESH


TOP_ACCURACY = lax.Precision.HIGHEST


def prefix(value, axis, join, neutral):
    count, mine = (lax.axis_size(axis), lax.axis_index(axis))
    pieces = lax.all_gather(value, axis)
    subtotal = jnp.full_like(value, 0) + jnp.asarray(neutral, value.dtype)

    def lap(position, subtotal):
        longer = join(subtotal, pieces[position])
        return jnp.where(position < mine, longer, subtotal)

    return lax.fori_loop(0, count - 1, lap, subtotal)


def shifted(block, axis, distance):
    devices = range(lax.axis_size(axis))
    route = [((i - distance) % len(devices), i) for i in devices]
    return lax.ppermute(block, axis, route)


def digits(indices):
    powers = LEVELS ** (TRANSMONS - 1 - jnp.arange(TRANSMONS, dtype=jnp.int32))
    return (indices[None, :] // powers[:, None] % LEVELS).astype(jnp.float32)


def energies(levels, level_shift, coupling):
    own_part = jnp.sum(level_shift[:, None] * levels * (levels - 1.0) * 0.5, axis=0)
    return own_part + jnp.sum(coupling[:, None] * levels[:-1] * levels[1:], axis=0)


def drift_tables(row_levels, col_levels, level_shift, coupling, dephase):
    detune_grid = (
        energies(row_levels, level_shift, coupling)[:, None]
        - energies(col_levels, level_shift, coupling)[None, :]
    )
    weighted = dephase[:, None] * row_levels
    cross = jnp.dot(
        weighted.T, col_levels, preferred_element_type=jnp.float32, precision=TOP_ACCURACY
    )
    row_part = jnp.sum(weighted * row_levels, axis=0)
    col_part = jnp.sum(dephase[:, None] * col_levels * col_levels, axis=0)
    decay = row_part[:, None] + col_part[None, :] - 2.0 * cross
    return (decay, detune_grid)


def half_factor(decay, detune_grid, span):
    magnitude = jnp.exp(-0.5 * span * decay)
    return (
        magnitude * jnp.cos(0.5 * span * detune_grid),
        -magnitude * jnp.sin(0.5 * span * detune_grid),
    )


def weigh(field, factor_real, factor_imag):
    return jnp.stack(
        [
            field[0] * factor_real - field[1] * factor_imag,
            field[0] * factor_imag + field[1] * factor_real,
        ]
    )


def complex_product(left_real_component, left_imaginary, right_real_component, right_imaginary):
    real_component = jnp.einsum(
        "nmx,nxw->nmw", left_real_component, right_real_component, precision=TOP_ACCURACY
    ) - jnp.einsum("nmx,nxw->nmw", left_imaginary, right_imaginary, precision=TOP_ACCURACY)
    imaginary_component = jnp.einsum(
        "nmx,nxw->nmw", left_real_component, right_imaginary, precision=TOP_ACCURACY
    ) + jnp.einsum("nmx,nxw->nmw", left_imaginary, right_real_component, precision=TOP_ACCURACY)
    return (real_component, imaginary_component)


def rotations(theta, phi):
    identity = jnp.eye(LEVELS, dtype=jnp.float32)
    total_real = jnp.broadcast_to(identity, (theta.shape[0], LEVELS, LEVELS))
    total_imag = jnp.zeros((theta.shape[0], LEVELS, LEVELS), jnp.float32)
    for level in range(LEVELS - 1):
        upper = jnp.outer(identity[level], identity[level + 1])
        lower = upper.T
        block = jnp.outer(identity[level], identity[level]) + jnp.outer(
            identity[level + 1], identity[level + 1]
        )
        cosine = jnp.cos(theta[:, level])[:, None, None]
        sine = jnp.sin(theta[:, level])[:, None, None]
        phase_cos = jnp.cos(phi[:, level])[:, None, None]
        phase_sin = jnp.sin(phi[:, level])[:, None, None]
        rot_real = identity + (cosine - 1.0) * block + sine * phase_cos * (lower - upper)
        rot_imag = sine * phase_sin * (upper + lower)
        total_real, total_imag = complex_product(total_real, total_imag, rot_real, rot_imag)
    return (total_real, total_imag)


def kron_range(unit_real, unit_imag, first, last):
    acc_real, acc_imag = (unit_real[first], unit_imag[first])
    for transmon in range(first + 1, last):
        next_real, next_imag = (unit_real[transmon], unit_imag[transmon])
        acc_real, acc_imag = (
            jnp.kron(acc_real, next_real) - jnp.kron(acc_imag, next_imag),
            jnp.kron(acc_real, next_imag) + jnp.kron(acc_imag, next_real),
        )
    return (acc_real, acc_imag)


def real_form(matrix_real, matrix_imag):
    return jnp.stack(
        [
            jnp.stack([matrix_real, -matrix_imag], axis=1),
            jnp.stack([matrix_imag, matrix_real], axis=1),
        ],
        axis=0,
    )


def factor_forms(unit_real, unit_imag):
    pairs = [
        kron_range(unit_real, unit_imag, 0, HALF),
        kron_range(unit_real, unit_imag, HALF, TRANSMONS),
    ]
    forward_left = [real_form(matrix_real, matrix_imag) for matrix_real, matrix_imag in pairs]
    forward_right = [real_form(matrix_real, -matrix_imag) for matrix_real, matrix_imag in pairs]
    adjoint_left = [real_form(matrix_real.T, -matrix_imag.T) for matrix_real, matrix_imag in pairs]
    adjoint_right = [real_form(matrix_real.T, matrix_imag.T) for matrix_real, matrix_imag in pairs]
    return (forward_left, forward_right, adjoint_left, adjoint_right)


def apply_factor(field, form, leading, trailing):
    width = form.shape[3]
    shaped = field.reshape(2, leading, width, trailing)
    result = jnp.einsum("cgdf,dpfq->cpgq", form, shaped, precision=TOP_ACCURACY)
    return result.reshape(field.shape)


def apply_factors(field, forms, leading, trailing):
    widths = [form.shape[3] for form in forms]
    for position, form in enumerate(forms):
        before = math.prod(widths[:position])
        after = math.prod(widths[position + 1 :])
        field = apply_factor(field, form, leading * before, after * trailing)
    return field


def step_unitaries(pulse, segment, clock, span, detuning):
    onehot = (jnp.arange(SEGMENTS, dtype=jnp.int32) == segment).astype(jnp.float32)
    theta = jnp.einsum("s,skm->km", onehot, pulse, precision=TOP_ACCURACY)
    multiple = jnp.arange(1, LEVELS, dtype=jnp.int32).astype(jnp.float32)
    phi = detuning[:, None] * (clock + 0.5 * span) * multiple[None, :]
    return rotations(theta, phi)


def sandwich(field, left_forms, right_forms):
    local_rows = field.shape[1]
    order_size = field.shape[2]
    members = lax.axis_size("row")
    block_width = order_size // members
    halfway = apply_factors(field, right_forms, local_rows, 1)
    halfway = halfway.reshape(2, local_rows, members, block_width)
    received = lax.all_to_all(halfway, "row", split_axis=2, concat_axis=1, tiled=True)
    count = received.shape[3]
    columns = apply_factors(received.reshape(2, order_size, count), left_forms, 1, count)
    turned = jnp.stack([columns[0].T, -columns[1].T])
    result = turned.reshape(2, 1, count, order_size)
    return result.reshape(2, block_width, order_size)


def local(linkage, pulse, segments, ticks, detuning, level_shift, coupling, dephase):
    current = linkage[:, 0]
    local_rows = current.shape[1]
    order_size = current.shape[2]
    row_rank = lax.axis_index("row")
    row_levels = digits(row_rank * local_rows + jnp.arange(local_rows, dtype=jnp.int32))
    col_levels = digits(jnp.arange(order_size, dtype=jnp.int32))
    decay, detune_grid = drift_tables(row_levels, col_levels, level_shift, coupling, dephase)
    step_ticks = ticks[0]

    def add_ticks(earlier, later):
        return earlier + later

    offsets = prefix(
        jnp.sum(step_ticks, keepdims=True, dtype=jnp.int32),
        "phase",
        add_ticks,
        jnp.zeros((1,), jnp.int32),
    )
    prepared = []
    for step_index in range(STEPS):
        span = step_ticks[step_index].astype(jnp.float32)
        clock = (offsets[0] + jnp.sum(step_ticks[:step_index], dtype=jnp.int32)).astype(jnp.float32)
        unit_real, unit_imag = step_unitaries(pulse, segments[0, step_index], clock, span, detuning)
        factor_real, factor_imag = half_factor(decay, detune_grid, span)
        prepared.append((factor_real, factor_imag, factor_forms(unit_real, unit_imag)))
    following = shifted(current, "phase", -1)
    field = current
    for forward_step_index in range(STEPS):
        forward_factor_real, forward_factor_imag, forward_forms = prepared[forward_step_index]
        field = weigh(field, forward_factor_real, forward_factor_imag)
        field = sandwich(field, forward_forms[0], forward_forms[1])
        field = weigh(field, forward_factor_real, forward_factor_imag)
    mismatch = field - following
    earlier_mismatch = shifted(mismatch, "phase", 1)
    adjoint = mismatch
    for step_index in reversed(range(STEPS)):
        factor_real, factor_imag, forms = prepared[step_index]
        adjoint = weigh(adjoint, factor_real, -factor_imag)
        adjoint = sandwich(adjoint, forms[2], forms[3])
        adjoint = weigh(adjoint, factor_real, -factor_imag)
    return (adjoint - earlier_mismatch)[:, None]


def dot3(left_high, left_low, right_high, right_low, contract_right=0):
    dims = (((1,), (contract_right,)), ((), ()))

    def one(left, right):
        return lax.dot_general(left, right, dims, preferred_element_type=jnp.float32)

    return one(left_high, right_high) + (one(left_high, right_low) + one(left_low, right_high))


def split(value):
    high = value.astype(jnp.bfloat16)
    return high, (value - high.astype(jnp.float32)).astype(jnp.bfloat16)


def rotation_cells(cosine, sine, k):
    def at(table, m):
        return table[k : k + 1, m : m + 1]

    rows = []
    for i in range(LEVELS):
        row = []
        for j in range(LEVELS):
            if i > j + 1:
                row.append(jnp.zeros((1, 1), jnp.float32))
            elif i == j + 1:
                row.append(at(sine, j))
            else:
                factors = [] if i == 0 else [at(cosine, i - 1)]
                factors += [-at(sine, m) for m in range(i, j)]
                factors += [] if j == LEVELS - 1 else [at(cosine, j)]
                row.append(math.prod(factors[1:], start=factors[0]))
        rows.append(row)
    return rows


def kernel(
    phases,
    members,
    ticks,
    segments,
    detuning,
    level_shift,
    coupling,
    dephase,
    tick_row,
    pulse,
    state,
    out,
    tick_rows,
    following,
    mismatch,
    earlier,
    first_high,
    first_low,
    second_high,
    second_low,
    sides,
    pre_table,
    mid_table,
    post_table,
    turned,
    gathered_high,
    gathered_low,
    halfway,
    send_one,
    receive_one,
    send_two,
    receive_two,
    send_sems,
    receive_sems,
    phase_sems,
    own_sems,
    tick_sems,
):
    phase = lax.axis_index("phase")
    me = lax.axis_index("row")
    rows, order = state.shape[1], state.shape[2]
    lead = LEVELS**HALF
    trail = order // lead
    count = trail // members
    lanes = lead * count
    per = lead // members
    cells = []
    for step in range(STEPS):
        theta = pulse[segments[0, step]]
        cosine, sine = jnp.cos(theta), jnp.sin(theta)
        cells.append([rotation_cells(cosine, sine, k) for k in range(TRANSMONS)])

    def q(step, k, i, j):
        return cells[step][k][i][j]

    def digit(index, k):
        return (index >> (2 * (TRANSMONS - 1 - k))) & (LEVELS - 1)

    barrier = pltpu.get_barrier_semaphore()
    after, before = lax.rem(phase + 1, phases), lax.rem(phase + phases - 1, phases)
    for offset in range(1, members):
        peer = lax.rem(me + offset, members)
        pl.semaphore_signal(barrier, inc=1, device_id=(phase, peer), device_id_type=MESH)
    for distance in range(1, phases):
        peer = lax.rem(phase + distance, phases)
        pl.semaphore_signal(barrier, inc=1, device_id=(peer, me), device_id_type=MESH)

    def pick(index, k, values):
        place = digit(index, k)
        result = jnp.where(place == 0, values[0], values[1])
        result = jnp.where(place == 2, values[2], result)
        return jnp.where(place == 3, values[3], result)

    def entries(row_index, col_index, k, step, swapped):
        vectors = []
        for i in range(LEVELS):
            values = [q(step, k, j, i) if swapped else q(step, k, i, j) for j in range(LEVELS)]
            vectors.append(pick(col_index, k, values))
        return pick(row_index, k, vectors)

    def kron_entries(row_index, col_index, ks, step, swapped):
        result = entries(row_index, col_index, ks[0], step, swapped)
        for k in ks[1:]:
            result = result * entries(row_index, col_index, k, step, swapped)
        return result

    head, tail = range(HALF), range(HALF, TRANSMONS)

    def iota(shape, axis):
        return lax.broadcasted_iota(jnp.int32, shape, axis)

    def build_dense(high, low, step, swapped):
        lane = iota((1, lanes), 1)
        lead_rows = [
            kron_entries(
                jnp.full((1, 1), a * trail, jnp.int32), (lane // count) * trail, head, step, swapped
            )
            for a in range(lead)
        ]
        for block in range(members):
            tile = kron_entries(
                iota((trail, 1), 0), block * count + lane % count, tail, step, swapped
            )
            for a in range(lead):
                upper, lower = split(tile * lead_rows[a])
                where = (slice(a * trail, (a + 1) * trail), slice(block * lanes, (block + 1) * lanes))
                high[where] = upper
                low[where] = lower

    def build_sides(step):
        row, col = iota((rows, 1), 0), iota((1, rows), 1)
        same = (row // trail) == (col // trail)
        lrow, lcol = iota((lanes, 1), 0), iota((1, lanes), 1)
        aligned = (lrow % count) == (lcol % count)
        for swapped in (False, True):
            body = kron_entries(row % trail, col % trail, tail, step, swapped)
            upper, lower = split(jnp.where(same, body, 0.0))
            base = 8 * step + 4 * swapped
            sides[base] = upper
            sides[base + 1] = lower
            body = kron_entries(
                (lrow // count) * trail, (lcol // count) * trail, head, step, swapped
            )
            upper, lower = split(jnp.where(aligned, body, 0.0))
            sides[base + 2] = upper
            sides[base + 3] = lower

    tau = [ticks[0, s].astype(jnp.float32) for s in range(STEPS)]

    def send_ticks():
        copies = []
        for distance in range(1, phases):
            copy = pltpu.make_async_remote_copy(
                src_ref=tick_row,
                dst_ref=tick_rows.at[phase],
                send_sem=tick_sems.at[0, distance],
                recv_sem=tick_sems.at[1, distance],
                device_id=(lax.rem(phase + distance, phases), me),
                device_id_type=MESH,
            )
            copy.start()
            copies.append(copy)
        return copies

    weights = []

    def set_weights():
        start = jnp.zeros((1, 1), jnp.int32)
        for distance in range(1, phases):
            row = tick_rows[lax.rem(phase + phases - distance, phases)]
            total = sum(row[:, s : s + 1] for s in range(STEPS))
            start = start + jnp.where(phase >= distance, total, 0)
        for s in range(STEPS):
            clock = start.astype(jnp.float32)
            weights.append([(clock + 0.5 * tau[s]) * detuning[k] for k in range(TRANSMONS)])
            start = start + ticks[0, s]

    def angle(index, which):
        n = [digit(index, k).astype(jnp.float32) for k in range(TRANSMONS)]
        energy = jnp.zeros(index.shape, jnp.float32)
        for k in range(TRANSMONS):
            energy = energy + level_shift[k] * (n[k] * (n[k] - 1.0) * 0.5)
        for k in range(TRANSMONS - 1):
            energy = energy + coupling[k] * (n[k] * n[k + 1])
        triangle = [v * (v + 1.0) * 0.5 for v in n]
        spin = [
            sum(weights[s][k] * triangle[k] for k in range(TRANSMONS))
            for s in range(STEPS)
        ]
        if which == 0:
            return -spin[0] - 0.5 * tau[0] * energy
        if which == 1:
            return (spin[0] - spin[1]) - 0.5 * (tau[0] + tau[1]) * energy
        return spin[1] - 0.5 * tau[1] * energy

    spans = (tau[0], tau[0] + tau[1], tau[1])

    def waves(index, which):
        value = angle(index, which)
        return jnp.cos(value), jnp.sin(value)

    def factor(row_index, col_index, row_waves, col_waves, which):
        decay = 0.0
        for k in range(TRANSMONS):
            gap = digit(row_index, k).astype(jnp.float32) - digit(col_index, k).astype(jnp.float32)
            decay = decay + dephase[k] * (gap * gap)
        size = jnp.exp(-0.5 * spans[which] * decay)
        row_cos, row_sin = row_waves
        col_cos, col_sin = col_waves
        return (
            size * (row_cos * col_cos + row_sin * col_sin),
            size * (row_sin * col_cos - row_cos * col_sin),
        )

    width = 128

    def build_row_table(table, which):
        row = me * rows + iota((rows, 1), 0)
        row_waves = waves(row, which)
        for chunk in range(order // width):
            col = chunk * width + iota((1, width), 1)
            real, imag = factor(row, col, row_waves, waves(col, which), which)
            table[0, :, pl.ds(chunk * width, width)] = real
            table[1, :, pl.ds(chunk * width, width)] = imag

    def build_mid_table():
        for block in range(members):
            other = lax.rem(me + members - block, members)
            lrow, lane = iota((lanes, 1), 0), iota((1, lanes), 1)
            row = (lrow // count) * trail + block * count + lrow % count
            col = (lane // count) * trail + other * count + lane % count
            real, imag = factor(row, col, waves(row, 1), waves(col, 1), 1)
            mid_table[0, block] = real
            mid_table[1, block] = imag

    def exchange(source, target, trip):
        copies = []
        for offset in range(1, members):
            peer = lax.rem(me + offset, members)
            copy = pltpu.make_async_remote_copy(
                src_ref=source.at[peer],
                dst_ref=target.at[me],
                send_sem=send_sems.at[trip, offset],
                recv_sem=receive_sems.at[trip, offset],
                device_id=(phase, peer),
                device_id_type=MESH,
            )
            copy.start()
            copies.append(copy)
        own = pltpu.make_async_copy(source.at[me], target.at[me], own_sems.at[trip])
        own.start()
        copies.append(own)
        return copies

    def hand(source, target, peer, number):
        copy = pltpu.make_async_remote_copy(
            src_ref=source,
            dst_ref=target,
            send_sem=phase_sems.at[0, number],
            recv_sem=phase_sems.at[1, number],
            device_id=(peer, me),
            device_id_type=MESH,
        )
        copy.start()
        return copy

    def outbound(read, sign, table, side, high, low, trip):
        left_high, left_low = sides[side], sides[side + 1]
        for chunk in range(order // width):
            where = pl.ds(chunk * width, width)
            straight, crossed = read(where)
            value = table[0, :, where] * straight + sign * (table[1, :, where] * crossed)
            moved = dot3(left_high, left_low, *split(value))
            upper, lower = split(moved)
            gathered_high[0:rows, where] = upper
            gathered_low[0:rows, where] = lower
        pack = 2
        for pair in range(members // pack):
            where = pl.ds(pair * pack * lanes, pack * lanes)
            moved = dot3(
                gathered_high[0:rows, :], gathered_low[0:rows, :], high[:, where], low[:, where]
            )
            for inner in range(pack):
                block = pair * pack + inner
                for b in range(members):
                    for part in range(per):
                        start = part * trail + b * count
                        send_one[trip // 3, (b + block) % members, start : start + count, :] = moved[
                            start : start + count, inner * lanes : (inner + 1) * lanes
                        ]
        return exchange(send_one.at[trip // 3], receive_one.at[trip // 3], trip)

    def middle(sign, first_side, second_side, trip):
        went = trip // 3
        for block in range(members):
            pieces = []
            for a in range(lead):
                start = (a % per) * trail + block * count
                pieces.append(receive_one[went, a // per, start : start + count, :])
            value = jnp.concatenate(pieces, axis=0)
            turned[block] = dot3(sides[first_side], sides[first_side + 1], *split(value))
        trips = []
        for kind in range(2):
            for block in range(members):
                other = lax.rem(me + members - block, members)
                straight = turned[block]
                crossed = turned[other].T
                real, imag = mid_table[0, block], sign * mid_table[1, block]
                if kind == 0:
                    value = real * straight + imag * crossed
                else:
                    value = real * crossed - imag * straight
                moved = dot3(sides[second_side], sides[second_side + 1], *split(value))
                for a in range(lead):
                    start = (a % per) * trail + block * count
                    send_two[went, kind, a // per, start : start + count, :] = moved[
                        a * count : (a + 1) * count, :
                    ]
            trips.append(
                exchange(send_two.at[went, kind], receive_two.at[went, kind], trip + kind)
            )
        return trips

    def inbound(side, high, low, went, kind):
        for block in range(members):
            pieces = []
            for part in range(per):
                for b in range(members):
                    start = part * trail + b * count
                    pieces.append(
                        receive_two[went, kind, (b + block) % members, start : start + count, :]
                    )
            upper, lower = split(jnp.concatenate(pieces, axis=0))
            where = (slice(0, rows), slice(block * lanes, (block + 1) * lanes))
            gathered_high[where] = upper
            gathered_low[where] = lower
        wide = 2 * width
        for chunk in range(order // wide):
            where = pl.ds(chunk * wide, wide)
            moved = dot3(
                gathered_high[0:rows, :], gathered_low[0:rows, :], high[where, :], low[where, :], 1
            )
            halfway[kind, :, where] = dot3(sides[side], sides[side + 1], *split(moved))

    def wait(copies):
        for copy in copies:
            copy.wait()

    pl.semaphore_wait(barrier, members + phases - 2)
    tick_copies = send_ticks()
    handed = hand(state, following, before, 0)
    build_dense(first_high, first_low, 0, True)
    build_sides(0)
    for copy in tick_copies:
        copy.wait()
    set_weights()
    build_row_table(pre_table, 0)

    def read_state(where):
        real, imag = state[0, :, where], state[1, :, where]
        return real + imag, real - imag

    copies = outbound(read_state, 1.0, pre_table, 0, first_high, first_low, 0)
    build_sides(1)
    build_mid_table()
    build_dense(second_high, second_low, 1, False)
    build_row_table(post_table, 2)
    wait(copies)
    trips = middle(1.0, 2, 10, 1)
    for kind in range(2):
        wait(trips[kind])
        inbound(8, second_high, second_low, 0, kind)
    handed.wait()
    for chunk in range(order // width):
        where = pl.ds(chunk * width, width)
        straight, crossed = halfway[0, :, where], halfway[1, :, where]
        real, imag = post_table[0, :, where], post_table[1, :, where]
        next_real, next_imag = following[0, :, where], following[1, :, where]
        mismatch[0, :, where] = real * straight + imag * crossed - (next_real + next_imag)
        mismatch[1, :, where] = real * crossed - imag * straight - (next_real - next_imag)

    def read_mismatch(where):
        return mismatch[0, :, where], mismatch[1, :, where]

    copies = outbound(read_mismatch, -1.0, post_table, 12, second_high, second_low, 3)
    handed = hand(mismatch, earlier, after, 1)
    wait(copies)
    trips = middle(-1.0, 14, 6, 4)
    for kind in range(2):
        wait(trips[kind])
        inbound(4, first_high, first_low, 1, kind)
    handed.wait()
    for chunk in range(order // width):
        where = pl.ds(chunk * width, width)
        straight, crossed = halfway[0, :, where], halfway[1, :, where]
        real, imag = pre_table[0, :, where], -pre_table[1, :, where]
        upper = real * straight + imag * crossed - earlier[0, :, where]
        lower = real * crossed - imag * straight - earlier[1, :, where]
        out[0, :, where] = 0.5 * (upper + lower)
        out[1, :, where] = 0.5 * (upper - lower)


def fused(linkage, pulse, segments, ticks, detuning, level_shift, coupling, dephase):
    phases, members = lax.axis_size("phase"), lax.axis_size("row")
    current = linkage[:, 0]
    rows, order = current.shape[1], current.shape[2]
    lanes = order // members
    full = (2, rows, order)
    one_way = (2, members, rows, lanes)
    two_way = (2, 2, members, rows, lanes)
    vmem = pl.BlockSpec(memory_space=pltpu.VMEM)
    result = pl.pallas_call(
        functools.partial(kernel, phases, members),
        out_shape=jax.ShapeDtypeStruct(full, jnp.float32),
        in_specs=[pl.BlockSpec(memory_space=pltpu.SMEM)] * 6 + [vmem] * 3,
        out_specs=vmem,
        scratch_shapes=[
            pltpu.VMEM((phases, 1, STEPS), jnp.int32),
            pltpu.VMEM(full, jnp.float32),
            pltpu.VMEM(full, jnp.float32),
            pltpu.VMEM(full, jnp.float32),
            pltpu.VMEM((order, order), jnp.bfloat16),
            pltpu.VMEM((order, order), jnp.bfloat16),
            pltpu.VMEM((order, order), jnp.bfloat16),
            pltpu.VMEM((order, order), jnp.bfloat16),
            pltpu.VMEM((8 * STEPS, rows, rows), jnp.bfloat16),
            pltpu.VMEM(full, jnp.float32),
            pltpu.VMEM((2, members, lanes, lanes), jnp.float32),
            pltpu.VMEM(full, jnp.float32),
            pltpu.VMEM((members, lanes, lanes), jnp.float32),
            pltpu.VMEM((rows, order), jnp.bfloat16),
            pltpu.VMEM((rows, order), jnp.bfloat16),
            pltpu.VMEM(full, jnp.float32),
            pltpu.VMEM(one_way, jnp.float32),
            pltpu.VMEM(one_way, jnp.float32),
            pltpu.VMEM(two_way, jnp.float32),
            pltpu.VMEM(two_way, jnp.float32),
            pltpu.SemaphoreType.DMA((6, members)),
            pltpu.SemaphoreType.DMA((6, members)),
            pltpu.SemaphoreType.DMA((2, 2)),
            pltpu.SemaphoreType.DMA((6,)),
            pltpu.SemaphoreType.DMA((2, phases)),
        ],
        compiler_params=pltpu.CompilerParams(
            collective_id=0, has_side_effects=True, vmem_limit_bytes=56 * 1024 * 1024
        ),
    )(ticks, segments, detuning, level_shift, coupling, dephase, ticks, pulse, current)
    return result[:, None]


def solution(mesh):
    members = mesh.shape["row"]
    trail = LEVELS ** (TRANSMONS - HALF)
    fits = STEPS == 2 and members <= LEVELS**HALF and LEVELS**HALF * (trail // members) == 128
    return jax.shard_map(
        fused if fits else local,
        mesh=mesh,
        in_specs=(
            P(None, "phase", "row", None),
            P(),
            P("phase", None),
            P("phase", None),
            P(),
            P(),
            P(),
            P(),
        ),
        out_specs=P(None, "phase", "row", None),
        check_vma=False,
    )
```
